32 devices in a mesh: dp: 4 (over y, x), expert: 8 (over z, core).
Axes of the slice: x: 2, y: 2, z: 4, core: 2. Of those that a mesh axis runs over, the one named last changes fastest.
Arguments:
- tokens: bfloat16 [4096, 2048], P(('dp', 'expert')), may hold values from -6 to 6
- out_grad: bfloat16 [4096, 2048], P(('dp', 'expert')), may hold values from -6 to 6
- routes: int32 [4096, 3], P(('dp', 'expert')), may hold values from 0 to 7, all different within a row; in each aligned block of 128 rows (0 to 127, 128 to 255, ...) at most 64 rows name the same one
- probs: bfloat16 [4096, 3], P(('dp', 'expert')), may hold values from 0.099609375 to 1
- w_in: bfloat16 [8, 2048, 1536], P('expert'), may hold values from -0.125 to 0.125
- w_out: bfloat16 [8, 768, 2048], P('expert'), may hold values from -0.21875 to 0.21875
Outputs:
- token_grad: bfloat16 [4096, 2048], P(('dp', 'expert'))
- prob_grad: bfloat16 [4096, 3], P(('dp', 'expert'))
- w_in_grad: bfloat16 [8, 2048, 1536], P('expert', 'dp')
- w_out_grad: bfloat16 [8, 768, 2048], P('expert', None, 'dp')
The draws below stay inside these ranges and needn't reach their ends.
Inputs may be any that keep to these rules, and one draw needn't show every extreme that they name: `routes`: each row names 3 different experts. In each device's aligned block of 128 rows no expert is named more than 64 times, a bound that some block reaches.
All inputs are finite; a program needn't handle non-finite values.
Results may differ from the reference program's by a relative error of at most 0.014.
Values may be sent and summed in bfloat16 or wider, within the bound.
A program may use at most 128 MiB of HBM per device.

```python
import math
import jax
import jax.numpy as jnp
import numpy as np
from jax import lax

D = 2048
F = 768
TOP = 3
TOK_DEV = 128
EXPERTS = 8
CAP = 64
TOKENS = 4096


def levels(own_key, shape, shards, least, high):
    level, own = 1.0, jax.random.fold_in(own_key, 6)
    for position, blocks in shards:
        draws = jnp.exp(jax.random.uniform(jax.random.fold_in(own, position), (blocks,), jnp.float32, least / len(shards), high / len(shards)))
        level = level * jnp.repeat(draws, shape[position] // blocks).reshape([-1 if axis == position else 1 for axis in range(len(shape))])
    return level


def deal_out(stream_key, own, number, rows, amount, top, limit, skew):
    order = jax.random.permutation(stream_key, amount)
    packed, usual = shares(amount, rows * top, limit, skew, True), shares(amount, rows * top, limit, skew, False)
    places = jnp.arange(amount)

    def named(tallies, offset_by):
        used = int((tallies > 0).sum())
        fixed = max(1, used // 4)
        shifted = fixed + (places - fixed + offset_by * (used - fixed)) % max(1, amount - fixed)
        return jnp.zeros((amount,), jnp.int32).at[order[jnp.where(places < fixed, places, shifted)]].set(jnp.asarray(tallies, jnp.int32))

    tallies = jnp.where(number % 4 == 0, named(packed, number // 4), named(usual, number - number // 4 - 1))
    mixed = jax.random.permutation(jax.random.fold_in(own, 3), amount)
    source_of, receiver = mixed[0:amount // 2 * 2:2], mixed[1:amount // 2 * 2:2]
    margin = jnp.minimum(tallies[source_of] - 1, limit - tallies[receiver]) // 2
    margin = jnp.where((source_of == order[0]) | (receiver == order[0]) | (tallies[receiver] == 0), 0, jnp.maximum(margin, 0))
    shifted = jax.random.randint(jax.random.fold_in(own, 4), (amount // 2,), 0, 1 << 20) % (margin + 1)
    tallies = tallies.at[source_of].add(-shifted).at[receiver].add(shifted)
    members = jnp.searchsorted(jnp.cumsum(tallies), jnp.arange(rows * top), side="right").astype(jnp.int32)
    listing = members.reshape(top, rows).T
    listing = listing[jax.random.permutation(jax.random.fold_in(own, 1), rows)]
    offset_by = jax.random.randint(jax.random.fold_in(own, 2), (rows, 1), 0, top)
    return jnp.take_along_axis(listing, (jnp.arange(top)[None, :] + offset_by) % top, axis=1)


def shares(count, total, most, skew, full):
    loads = [(1 << 20) // math.isqrt(standing ** skew) + 1 for standing in range(1, count + 1)]
    largest = most if full else min(most, max(-(-total // count), total * loads[0] // sum(loads)))
    least = 1 if total - largest >= count - 1 else 0
    holding, spare = [largest] + [least] * (count - 1), total - largest - least * (count - 1)
    while spare > 0:
        movable = [i for i in range(1, count) if holding[i] < largest] or [i for i in range(1, count) if holding[i] < most]
        whole, remaining = sum([loads[i] for i in movable]), spare
        for i in movable:
            extra = min(most - holding[i], max(1, remaining * loads[i] // whole), spare)
            holding[i] = holding[i] + extra
            spare = spare - extra
    return np.array(holding)


def noise(stream_key, shape, spread, limit, pieces=(), kind=jnp.bfloat16):
    gain = levels(stream_key, shape, pieces, -0.22, 0.18) if pieces else 1.0
    entries = jax.random.normal(stream_key, shape, jnp.float32) * spread * gain
    return jnp.minimum(jnp.maximum(entries, -limit), limit).astype(kind)


def setup_inputs(seed: int = 0) -> dict:
    seeds = jax.random.split(jax.random.key(seed), 7)
    tokens = noise(seeds[0], (TOKENS, D), 1.0, 6.0, ((0, 32),))
    out_grad = noise(seeds[1], (TOKENS, D), 1.0, 6.0, ((0, 32),))
    routes_keys = jax.random.split(jax.random.fold_in(seeds[2], 1), TOKENS // TOK_DEV)
    routes_turns = jax.random.permutation(jax.random.fold_in(seeds[2], 3), TOKENS // TOK_DEV)
    routes = jax.vmap(lambda own, number: deal_out(jax.random.fold_in(seeds[2], 2), own, number, TOK_DEV, EXPERTS, TOP, CAP, 2))(routes_keys, routes_turns).reshape((TOKENS, TOP))
    probs = jnp.clip(jnp.exp(math.log(1.0) - 2.306499 * jax.random.uniform(seeds[3], (TOKENS, TOP), jnp.float32) ** levels(seeds[3], (TOKENS, TOP), ((0, 32),), -0.2, 0.2)), 0.099609375, 1.0).astype(jnp.bfloat16)
    w_in = noise(seeds[4], (EXPERTS, D, 2 * F), D ** -0.5, 0.125, ((0, 8),))
    w_out = noise(seeds[5], (EXPERTS, F, D), F ** -0.5, 0.21875, ((0, 8),))
    return {"tokens": tokens, "out_grad": out_grad, "routes": routes, "probs": probs, "w_in": w_in, "w_out": w_out}


def silu_parts(gate):
    sig = jax.nn.sigmoid(gate)
    return gate * sig, sig * (1.0 + gate * (1.0 - sig))


def reference(tokens, out_grad, routes, probs, w_in, w_out):
    flat = routes.reshape(-1).astype(jnp.int32)
    maxrows = CAP * (TOKENS // TOK_DEV)
    order = jnp.argsort(flat, stable=True).astype(jnp.int32)
    counts = jnp.sum((flat[:, None] == jnp.arange(EXPERTS, dtype=jnp.int32)[None, :]).astype(jnp.int32), axis=0)
    offsets = (jnp.cumsum(counts) - counts).astype(jnp.int32)
    padded = jnp.concatenate([order, jnp.zeros((maxrows,), jnp.int32)])
    probs_flat = probs.reshape(-1)

    def per_expert(carry, inputs):
        grad_acc, prob_acc = carry
        w_one, w_two, offset, total = inputs
        index = lax.dynamic_slice(padded, (offset.astype(jnp.int32),), (maxrows,))
        valid = jnp.arange(maxrows, dtype=jnp.int32) < total
        source = index // TOP
        rows_x = jnp.where(valid[:, None], tokens[source], jnp.zeros((), tokens.dtype))
        rows_dy = jnp.where(valid[:, None], out_grad[source], jnp.zeros((), out_grad.dtype))
        rows_p = jnp.where(valid, probs_flat[index], jnp.zeros((), probs.dtype))
        proj = jnp.dot(rows_x, w_one, preferred_element_type=jnp.float32)
        gate, upper = proj[:, :F], proj[:, F:]
        act, slope = silu_parts(gate)
        hid = (act * upper).astype(jnp.bfloat16)
        outs = jnp.dot(hid, w_two, preferred_element_type=jnp.float32).astype(jnp.bfloat16)
        dprob = jnp.sum(rows_dy.astype(jnp.float32) * outs.astype(jnp.float32), axis=1).astype(jnp.bfloat16)
        slot_grad = (rows_p.astype(jnp.float32)[:, None] * rows_dy.astype(jnp.float32)).astype(jnp.bfloat16)
        hid_grad = jnp.dot(slot_grad, w_two.T, preferred_element_type=jnp.float32)
        proj_grad = jnp.concatenate([hid_grad * upper * slope, hid_grad * act], axis=1).astype(jnp.bfloat16)
        row_grad = jnp.dot(proj_grad, w_one.T, preferred_element_type=jnp.float32).astype(jnp.bfloat16)
        grad_one = lax.dot_general(rows_x, proj_grad, (((0,), (0,)), ((), ())), preferred_element_type=jnp.float32)
        grad_two = lax.dot_general(hid, slot_grad, (((0,), (0,)), ((), ())), preferred_element_type=jnp.float32)
        grad_acc = grad_acc.at[source].add(jnp.where(valid[:, None], row_grad.astype(jnp.float32), jnp.float32(0.0)))
        prob_acc = prob_acc.at[index].add(jnp.where(valid, dprob.astype(jnp.float32), jnp.float32(0.0)))
        return (grad_acc, prob_acc), (grad_one.astype(jnp.bfloat16), grad_two.astype(jnp.bfloat16))

    start = (jnp.zeros((TOKENS, D), jnp.float32), jnp.zeros((TOKENS * TOP,), jnp.float32))
    (grad_acc, prob_acc), (w_in_grad, w_out_grad) = lax.scan(per_expert, start, (w_in, w_out, offsets, counts))
    return (grad_acc.astype(jnp.bfloat16), prob_acc.reshape(TOKENS, TOP).astype(jnp.bfloat16), w_in_grad, w_out_grad)
```

```python
import jax
import jax.numpy as jnp
from jax import lax
from jax.sharding import PartitionSpec as P

F32 = jnp.float32
BF16 = jnp.bfloat16


def exclusive_rank(hits):
    rows = hits.shape[1]
    earlier = (jnp.arange(rows)[:, None] < jnp.arange(rows)[None, :]).astype(BF16)
    return jnp.dot(hits.astype(BF16), earlier, preferred_element_type=F32)


def dispatch_gather(tokens, out_grad, routes, probs, cap):
    tok_rows, width = tokens.shape
    top = routes.shape[1]
    me = lax.axis_index("expert").astype(F32)
    table = jnp.concatenate([routes.T.astype(BF16), probs.T], axis=0)
    table = lax.all_gather(table, "expert", axis=0, tiled=False).astype(F32)
    all_x = lax.all_gather(tokens, "expert", axis=0, tiled=False)
    all_dy = lax.all_gather(out_grad, "expert", axis=0, tiled=False)
    mine = table[:, :top] == me
    hits = jnp.any(mine, axis=1)
    prob = jnp.sum(jnp.where(mine, table[:, top:], 0.0), axis=1)
    rank = exclusive_rank(hits)
    place = (rank[:, None, :] == jnp.arange(cap, dtype=F32)[None, :, None]) & hits[:, None, :]
    pick = place.astype(BF16)
    rows_p = jnp.sum(jnp.where(place, prob[:, None, :], 0.0), axis=2).reshape(-1)

    def take(rows):
        out = lax.dot_general(pick, rows, (((2,), (1,)), ((0,), (0,))), preferred_element_type=F32)
        return out.astype(BF16).reshape(-1, width)

    return take(all_x), take(all_dy), rows_p


def dispatch_exchange(tokens, out_grad, probs, slot, experts, cap):
    tok_rows, width = tokens.shape
    top = slot.shape[1]
    flat = slot.reshape(-1)
    slot_hit = flat[:, None] == jnp.arange(experts * cap, dtype=jnp.int32)[None, :]
    filled = jnp.any(slot_hit, axis=0)
    owner = jnp.sum(jnp.where(slot_hit, jnp.arange(flat.shape[0], dtype=jnp.int32)[:, None], 0), axis=0)
    source = owner // top
    zero = jnp.zeros((), BF16)

    def move(rows):
        return lax.all_to_all(rows, "expert", split_axis=0, concat_axis=0, tiled=True)

    send_x = jnp.where(filled[:, None], tokens[source], zero).reshape(experts, cap, width)
    send_dy = jnp.where(filled[:, None], out_grad[source], zero).reshape(experts, cap, width)
    send_p = jnp.where(filled, probs.reshape(-1)[owner], zero).reshape(experts, cap)
    return (
        move(send_x).reshape(-1, width),
        move(send_dy).reshape(-1, width),
        move(send_p).reshape(-1).astype(F32),
    )


def shards(tokens, out_grad, routes, probs, w_in, w_out):
    tok_rows, width = tokens.shape
    top = routes.shape[1]
    n_groups = lax.axis_size("expert")
    experts = n_groups * w_in.shape[0]
    hidden = w_out.shape[1]
    cap = 4 * tok_rows * top // (3 * experts)
    w_one, w_two = w_in[0], w_out[0]

    names = jnp.arange(experts, dtype=jnp.int32)
    named = routes[:, :, None] == names[None, None, :]
    hits = jnp.any(named, axis=1)
    later = (jnp.arange(tok_rows)[:, None] > jnp.arange(tok_rows)[None, :]).astype(BF16)
    rank = jnp.dot(later, hits.astype(BF16), preferred_element_type=F32)
    own_rank = jnp.sum(jnp.where(named, rank[:, None, :], 0.0), axis=2).astype(jnp.int32)
    slot = routes * cap + own_rank

    if experts <= 16:
        rows_x, rows_dy, rows_p = dispatch_gather(tokens, out_grad, routes, probs, cap)
    else:
        rows_x, rows_dy, rows_p = dispatch_exchange(tokens, out_grad, probs, slot, experts, cap)
    rows_p = rows_p[:, None]

    proj = jnp.dot(rows_x, w_one, preferred_element_type=F32)
    gate, upper = proj[:, :hidden], proj[:, hidden:]
    sig = jax.nn.sigmoid(gate)
    act = gate * sig
    hid = (act * upper).astype(BF16)
    scaled = (rows_p * hid.astype(F32)).astype(BF16)
    contract = (((0,), (0,)), ((), ()))
    grad_two = lax.dot_general(scaled, rows_dy, contract, preferred_element_type=F32).astype(BF16)
    share_two = lax.psum_scatter(grad_two, "dp", scatter_dimension=1, tiled=True)

    back = lax.dot_general(rows_dy, w_two, (((1,), (1,)), ((), ())), preferred_element_type=F32)
    dprob = jnp.sum(back * hid.astype(F32), axis=1).astype(BF16)
    hid_grad = rows_p * back
    proj_grad = jnp.concatenate(
        [hid_grad * upper * (sig * (1.0 + gate * (1.0 - sig))), hid_grad * act], axis=1
    ).astype(BF16)
    grad_one = lax.dot_general(rows_x, proj_grad, contract, preferred_element_type=F32).astype(BF16)
    share_one = lax.psum_scatter(grad_one, "dp", scatter_dimension=0, tiled=True)

    row_grad = lax.dot_general(
        proj_grad, w_one, (((1,), (1,)), ((), ())), preferred_element_type=F32
    ).astype(BF16)
    back_x = lax.all_to_all(
        row_grad.reshape(n_groups, cap, width), "expert", split_axis=0, concat_axis=0, tiled=True
    ).reshape(experts * cap, width)
    back_p = lax.all_to_all(
        dprob.reshape(n_groups, cap), "expert", split_axis=0, concat_axis=0, tiled=True
    ).reshape(-1)
    slots = jnp.arange(experts * cap, dtype=jnp.int32)
    held = slot[:, :, None] == slots[None, None, :]
    prob_grad = jnp.sum(jnp.where(held, back_p.astype(F32), 0.0), axis=2).astype(BF16)
    token_grad = jnp.dot(
        jnp.any(held, axis=1).astype(BF16), back_x, preferred_element_type=F32
    ).astype(BF16)
    return token_grad, prob_grad, share_one[None], share_two[None]


def solution(mesh):
    return jax.shard_map(
        shards,
        mesh=mesh,
        in_specs=(
            P(("dp", "expert"), None),
            P(("dp", "expert"), None),
            P(("dp", "expert"), None),
            P(("dp", "expert"), None),
            P("expert", None, None),
            P("expert", None, None),
        ),
        out_specs=(
            P(("dp", "expert"), None),
            P(("dp", "expert"), None),
            P("expert", "dp", None),
            P("expert", None, "dp"),
        ),
        check_vma=False,
    )
```

```python
import jax
import jax.numpy as jnp
from jax import lax
from jax.experimental import pallas as pl
from jax.experimental.pallas import tpu as pltpu
from jax.sharding import PartitionSpec as P

F32 = jnp.float32
BF16 = jnp.bfloat16


def gather_kernel(n, *refs):
    count = 3
    ins, outs = refs[:count], refs[count : 2 * count]
    own_sem, send_sem, recv_sem = refs[2 * count :]
    chips = n // 2
    me = lax.axis_index("expert")
    z, core = me // 2, me % 2
    ways = (
        (me - core + 1 - core, None),
        (me + 2, z < chips - 1),
        (me - 2, z > 0),
    )

    def guarded(ok, body):
        if ok is None:
            body()
        else:
            pl.when(ok)(body)

    barrier = pltpu.get_barrier_semaphore()
    for target, ok in ways:
        guarded(ok, lambda target=target: pl.semaphore_signal(
            barrier, inc=1, device_id={"expert": target}, device_id_type=pl.DeviceIdType.MESH
        ))
    peers = 1 + (z < chips - 1).astype(jnp.int32) + (z > 0).astype(jnp.int32)
    pl.semaphore_wait(barrier, peers)

    def copy(a, slot, hop, way):
        source = ins[a] if hop is None else outs[a].at[slot]
        return pltpu.make_async_remote_copy(
            src_ref=source,
            dst_ref=outs[a].at[slot],
            send_sem=send_sem.at[a, 0 if hop is None else hop, way],
            recv_sem=recv_sem.at[a, slot],
            device_id={"expert": ways[way][0]},
            device_id_type=pl.DeviceIdType.MESH,
        )

    def locals_():
        return [pltpu.make_async_copy(ins[a], outs[a].at[me], own_sem.at[a]) for a in range(count)]

    for a in range(count):
        for way in (1, 2, 0):
            guarded(ways[way][1], lambda a=a, way=way: copy(a, me, None, way).start())
    for c in locals_():
        c.start()
    hops = []
    for step in range(1, chips):
        hops.append((2 * step - 1, me - 2 * step, z - step >= 0, 1))
        hops.append((2 * step, me + 2 * step, z + step < chips, 2))
    for step in range(chips - 1):
        for a in range(count):
            for hop, slot, here, way in hops[2 * step : 2 * step + 2]:

                def relay(a=a, hop=hop, slot=slot, way=way):
                    copy(a, slot, hop, way).wait_recv()
                    pl.when(ways[way][1])(lambda: copy(a, slot, hop, way).start())
                    copy(a, slot, hop, 0).start()

                pl.when(here)(relay)
    for a in range(count):
        for chip in range(chips):
            copy(a, 2 * chip + 1 - core, 0, 0).wait_recv()
    for c in locals_():
        c.wait()
    for a in range(count):
        for way in range(3):
            guarded(ways[way][1], lambda a=a, way=way: copy(a, me, None, way).wait_send())
        for hop, slot, here, way in hops:

            def drain(a=a, hop=hop, slot=slot, way=way):
                pl.when(ways[way][1])(lambda: copy(a, slot, hop, way).wait_send())
                copy(a, slot, hop, 0).wait_send()

            pl.when(here)(drain)


def gather_all(n, *arrays):
    return pl.pallas_call(
        lambda *refs: gather_kernel(n, *refs),
        out_shape=[jax.ShapeDtypeStruct((n,) + a.shape, a.dtype) for a in arrays],
        in_specs=[pl.BlockSpec(memory_space=pltpu.VMEM)] * len(arrays),
        out_specs=[pl.BlockSpec(memory_space=pl.ANY)] * len(arrays),
        scratch_shapes=[
            pltpu.SemaphoreType.DMA((len(arrays),)),
            pltpu.SemaphoreType.DMA((len(arrays), n - 1, 3)),
            pltpu.SemaphoreType.DMA((len(arrays), n)),
        ],
        compiler_params=pltpu.CompilerParams(collective_id=0, has_side_effects=True),
    )(*arrays)


def exclusive_rank(hits):
    rows = hits.shape[1]
    earlier = (jnp.arange(rows)[:, None] < jnp.arange(rows)[None, :]).astype(BF16)
    return jnp.dot(hits.astype(BF16), earlier, preferred_element_type=F32)


def dispatch_gather(tokens, out_grad, routes, probs, cap):
    tok_rows, width = tokens.shape
    top = routes.shape[1]
    me = lax.axis_index("expert").astype(F32)
    table = jnp.concatenate([routes.T.astype(BF16), probs.T], axis=0)
    table = jnp.pad(table, ((0, -2 * top % 16), (0, 0)))
    table, all_x, all_dy = gather_all(lax.axis_size("expert"), table, tokens, out_grad)
    table = table.astype(F32)
    mine = table[:, :top] == me
    hits = jnp.any(mine, axis=1)
    prob = jnp.sum(jnp.where(mine, table[:, top : 2 * top], 0.0), axis=1)
    rank = exclusive_rank(hits)
    place = (rank[:, None, :] == jnp.arange(cap, dtype=F32)[None, :, None]) & hits[:, None, :]
    pick = place.astype(BF16)
    rows_p = jnp.sum(jnp.where(place, prob[:, None, :], 0.0), axis=2).reshape(-1)

    def take(rows):
        out = lax.dot_general(pick, rows, (((2,), (1,)), ((0,), (0,))), preferred_element_type=F32)
        return out.astype(BF16).reshape(-1, width)

    return take(all_x), take(all_dy), rows_p


def dispatch_exchange(tokens, out_grad, probs, slot, experts, cap):
    tok_rows, width = tokens.shape
    top = slot.shape[1]
    flat = slot.reshape(-1)
    slot_hit = flat[:, None] == jnp.arange(experts * cap, dtype=jnp.int32)[None, :]
    filled = jnp.any(slot_hit, axis=0)
    owner = jnp.sum(jnp.where(slot_hit, jnp.arange(flat.shape[0], dtype=jnp.int32)[:, None], 0), axis=0)
    source = owner // top
    zero = jnp.zeros((), BF16)

    def move(rows):
        return lax.all_to_all(rows, "expert", split_axis=0, concat_axis=0, tiled=True)

    send_x = jnp.where(filled[:, None], tokens[source], zero).reshape(experts, cap, width)
    send_dy = jnp.where(filled[:, None], out_grad[source], zero).reshape(experts, cap, width)
    send_p = jnp.where(filled, probs.reshape(-1)[owner], zero).reshape(experts, cap)
    return (
        move(send_x).reshape(-1, width),
        move(send_dy).reshape(-1, width),
        move(send_p).reshape(-1).astype(F32),
    )


def swap(value, flip):
    return lax.ppermute(value, "dp", [(i, i ^ flip) for i in range(4)])


def square_first(piece):
    got = []
    for rest in (True, False):
        for half, side in ((0, 1), (1, 2)):
            flip = 3 if rest else side
            got.append(swap(piece(flip, half).astype(BF16), side))
    return got


def square_second(piece, got):
    sent = []
    for half, side in ((0, 2), (1, 1)):
        total = (piece(side, half) + got[half].astype(F32)).astype(BF16)
        sent.append(swap(total, side))
    return [
        (piece(0, half) + got[2 + half].astype(F32) + sent[half].astype(F32)).astype(BF16)
        for half in range(2)
    ]


def shards(tokens, out_grad, routes, probs, w_in, w_out):
    tok_rows, width = tokens.shape
    top = routes.shape[1]
    n_groups = lax.axis_size("expert")
    experts = n_groups * w_in.shape[0]
    hidden = w_out.shape[1]
    cap = 4 * tok_rows * top // (3 * experts)
    w_one, w_two = w_in[0], w_out[0]

    names = jnp.arange(experts, dtype=jnp.int32)
    named = routes[:, :, None] == names[None, None, :]
    hits = jnp.any(named, axis=1)
    later = (jnp.arange(tok_rows)[:, None] > jnp.arange(tok_rows)[None, :]).astype(BF16)
    rank = jnp.dot(later, hits.astype(BF16), preferred_element_type=F32)
    own_rank = jnp.sum(jnp.where(named, rank[:, None, :], 0.0), axis=2).astype(jnp.int32)
    slot = routes * cap + own_rank

    if experts <= 16:
        rows_x, rows_dy, rows_p = dispatch_gather(tokens, out_grad, routes, probs, cap)
    else:
        rows_x, rows_dy, rows_p = dispatch_exchange(tokens, out_grad, probs, slot, experts, cap)
    rows_p = rows_p[:, None]

    proj = jnp.dot(rows_x, w_one, preferred_element_type=F32)
    gate, upper = proj[:, :hidden], proj[:, hidden:]
    sig = jax.nn.sigmoid(gate)
    act = gate * sig
    hid = (act * upper).astype(BF16)
    scaled = (rows_p * hid.astype(F32)).astype(BF16)
    replicas = lax.axis_size("dp")
    part = width // replicas
    at = lax.axis_index("dp")
    contract = (((0,), (0,)), ((), ()))

    def piece_two(flip, half):
        cut = lax.dynamic_slice_in_dim(rows_dy, (at ^ flip) * part, part, axis=1)
        units = scaled[:, half * (hidden // 2) : (half + 1) * (hidden // 2)]
        return lax.dot_general(units, cut, contract, preferred_element_type=F32)

    if replicas == 4:
        first_two = square_first(piece_two)
    else:
        grad_two = lax.dot_general(scaled, rows_dy, contract, preferred_element_type=F32).astype(BF16)
        share_two = lax.psum_scatter(grad_two, "dp", scatter_dimension=1, tiled=True)

    back = lax.dot_general(rows_dy, w_two, (((1,), (1,)), ((), ())), preferred_element_type=F32)
    dprob = jnp.sum(back * hid.astype(F32), axis=1).astype(BF16)
    hid_grad = rows_p * back
    proj_grad = jnp.concatenate(
        [hid_grad * upper * (sig * (1.0 + gate * (1.0 - sig))), hid_grad * act], axis=1
    ).astype(BF16)

    def piece_one(flip, half):
        cut = lax.dynamic_slice_in_dim(rows_x, (at ^ flip) * part, part, axis=1)
        units = proj_grad[:, half * hidden : (half + 1) * hidden]
        return lax.dot_general(cut, units, contract, preferred_element_type=F32)

    if replicas == 4:
        first_one = square_first(piece_one)
        second_two = square_second(piece_two, first_two)
        second_one = square_second(piece_one, first_one)
        share_two = jnp.concatenate(second_two, axis=0)
        share_one = jnp.concatenate(second_one, axis=1)
    else:
        grad_one = lax.dot_general(rows_x, proj_grad, contract, preferred_element_type=F32).astype(BF16)
        share_one = lax.psum_scatter(grad_one, "dp", scatter_dimension=0, tiled=True)

    row_grad = lax.dot_general(
        proj_grad, w_one, (((1,), (1,)), ((), ())), preferred_element_type=F32
    ).astype(BF16)
    back_x = lax.all_to_all(
        row_grad.reshape(n_groups, cap, width), "expert", split_axis=0, concat_axis=0, tiled=True
    ).reshape(experts * cap, width)
    back_p = lax.all_to_all(
        dprob.reshape(n_groups, cap), "expert", split_axis=0, concat_axis=0, tiled=True
    ).reshape(-1)
    slots = jnp.arange(experts * cap, dtype=jnp.int32)
    held = slot[:, :, None] == slots[None, None, :]
    prob_grad = jnp.sum(jnp.where(held, back_p.astype(F32), 0.0), axis=2).astype(BF16)
    token_grad = jnp.dot(
        jnp.any(held, axis=1).astype(BF16), back_x, preferred_element_type=F32
    ).astype(BF16)
    return token_grad, prob_grad, share_one[None], share_two[None]


def solution(mesh):
    return jax.shard_map(
        shards,
        mesh=mesh,
        in_specs=(
            P(("dp", "expert"), None),
            P(("dp", "expert"), None),
            P(("dp", "expert"), None),
            P(("dp", "expert"), None),
            P("expert", None, None),
            P("expert", None, None),
        ),
        out_specs=(
            P(("dp", "expert"), None),
            P(("dp", "expert"), None),
            P("expert", "dp", None),
            P("expert", None, "dp"),
        ),
        check_vma=False,
    )
```

```python
import jax
import jax.numpy as jnp
from jax import lax
from jax.experimental import pallas as pl
from jax.experimental.pallas import tpu as pltpu
from jax.sharding import PartitionSpec as P

F32 = jnp.float32
BF16 = jnp.bfloat16


def gather_kernel(n, cap, top, *refs):
    count = 3
    ins, w_hbm = refs[:count], refs[count]
    table_out, rows_x, rows_dy, proj = refs[count + 1 : count + 5]
    all_x, all_dy, w_vmem, w_sem, own_sem, send_sem, recv_sem = refs[count + 5 :]
    outs = (table_out, all_x, all_dy)
    load_w = pltpu.make_async_copy(w_hbm, w_vmem, w_sem)
    load_w.start()
    chips = n // 2
    me = lax.axis_index("expert")
    z, core = me // 2, me % 2
    ways = (
        (me - core + 1 - core, None),
        (me + 2, z < chips - 1),
        (me - 2, z > 0),
    )

    def guarded(ok, body):
        if ok is None:
            body()
        else:
            pl.when(ok)(body)

    barrier = pltpu.get_barrier_semaphore()
    for target, ok in ways:
        guarded(ok, lambda target=target: pl.semaphore_signal(
            barrier, inc=1, device_id={"expert": target}, device_id_type=pl.DeviceIdType.MESH
        ))
    peers = 1 + (z < chips - 1).astype(jnp.int32) + (z > 0).astype(jnp.int32)
    pl.semaphore_wait(barrier, peers)

    def copy(a, slot, hop, way):
        source = ins[a] if hop is None else outs[a].at[slot]
        return pltpu.make_async_remote_copy(
            src_ref=source,
            dst_ref=outs[a].at[slot],
            send_sem=send_sem.at[a, 0 if hop is None else hop, way],
            recv_sem=recv_sem.at[a, slot],
            device_id={"expert": ways[way][0]},
            device_id_type=pl.DeviceIdType.MESH,
        )

    def locals_():
        return [pltpu.make_async_copy(ins[a], outs[a].at[me], own_sem.at[a]) for a in range(count)]

    for c in locals_():
        c.start()
    hops = []
    for step in range(1, chips):
        hops.append((2 * step - 1, me - 2 * step, z - step >= 0, 1))
        hops.append((2 * step, me + 2 * step, z + step < chips, 2))
    def pick(rows_in, rows_out):
        tok = rows_in.shape[1]
        earlier = (
            lax.broadcasted_iota(jnp.int32, (tok, tok), 0) < lax.broadcasted_iota(jnp.int32, (tok, tok), 1)
        )
        earlier = jnp.where(earlier, 1.0, 0.0).astype(BF16)
        order = lax.broadcasted_iota(jnp.int32, (cap, tok), 0).astype(F32)

        def one(b, carry):
            named = table_out[b].astype(F32)
            hit = jnp.zeros((1, tok), F32)
            for k in range(top):
                hit = hit + jnp.where(named[k : k + 1] == me.astype(F32), 1.0, 0.0)
            rank = jnp.dot(
                jnp.broadcast_to(hit, (16, tok)).astype(BF16), earlier, preferred_element_type=F32
            )[0:1]
            place = jnp.where(order == rank, 1.0, 0.0) * hit
            rows_out[pl.ds(pl.multiple_of(b * cap, cap), cap), :] = jnp.dot(
                place.astype(BF16), rows_in[b], preferred_element_type=F32
            ).astype(BF16)
            return carry

        lax.fori_loop(0, n, one, 0)

    def send_own(a):
        for way in (1, 2, 0):
            guarded(ways[way][1], lambda a=a, way=way: copy(a, me, None, way).start())

    def pass_on(a):
        for hop, slot, here, way in hops:

            def relay(a=a, hop=hop, slot=slot, way=way):
                copy(a, slot, hop, way).wait_recv()
                pl.when(ways[way][1])(lambda: copy(a, slot, hop, way).start())
                copy(a, slot, hop, 0).start()

            pl.when(here)(relay)

    def finish(a):
        for chip in range(chips):
            copy(a, 2 * chip + 1 - core, 0, 0).wait_recv()

    send_own(0)
    send_own(1)
    pass_on(0)
    pass_on(1)
    send_own(2)
    for c in locals_():
        c.wait()
    finish(0)
    finish(1)
    load_w.wait()
    tile = 256
    steps = proj.shape[1] // tile
    width = steps // len(hops) if steps >= len(hops) else 0

    def columns(first, last):
        def one(i, carry):
            at = pl.ds(pl.multiple_of(i * tile, tile), tile)
            proj[:, at] = jnp.dot(rows_x[...], w_vmem[:, at], preferred_element_type=F32)
            return carry

        lax.fori_loop(first, last, one, 0)

    pick(all_x, rows_x)
    for i, (hop, slot, here, way) in enumerate(hops):

        def relay(hop=hop, slot=slot, way=way):
            copy(2, slot, hop, way).wait_recv()
            pl.when(ways[way][1])(lambda: copy(2, slot, hop, way).start())
            copy(2, slot, hop, 0).start()

        pl.when(here)(relay)
        columns(i * width, (i + 1) * width if i < len(hops) - 1 else steps)
    finish(2)
    pick(all_dy, rows_dy)
    for a in range(count):
        for way in range(3):
            guarded(ways[way][1], lambda a=a, way=way: copy(a, me, None, way).wait_send())
        for hop, slot, here, way in hops:

            def drain(a=a, hop=hop, slot=slot, way=way):
                pl.when(ways[way][1])(lambda: copy(a, slot, hop, way).wait_send())
                copy(a, slot, hop, 0).wait_send()

            pl.when(here)(drain)


def gather_all(n, cap, top, w_one, *arrays):
    table, rows = arrays[:2]
    vmem, width = pl.BlockSpec(memory_space=pltpu.VMEM), rows.shape[1]
    return pl.pallas_call(
        lambda *refs: gather_kernel(n, cap, top, *refs),
        out_shape=[
            jax.ShapeDtypeStruct((n,) + table.shape, BF16),
            jax.ShapeDtypeStruct((n * cap, width), BF16),
            jax.ShapeDtypeStruct((n * cap, width), BF16),
            jax.ShapeDtypeStruct((n * cap, w_one.shape[1]), F32),
        ],
        in_specs=[vmem] * 3 + [pl.BlockSpec(memory_space=pl.ANY)],
        out_specs=[vmem] * 4,
        scratch_shapes=[
            pltpu.VMEM((n,) + rows.shape, BF16),
            pltpu.VMEM((n,) + rows.shape, BF16),
            pltpu.VMEM(w_one.shape, BF16),
            pltpu.SemaphoreType.DMA,
            pltpu.SemaphoreType.DMA((3,)),
            pltpu.SemaphoreType.DMA((3, n - 1, 3)),
            pltpu.SemaphoreType.DMA((3, n)),
        ],
        compiler_params=pltpu.CompilerParams(
            collective_id=0, has_side_effects=True, vmem_limit_bytes=48 * 1024 * 1024
        ),
    )(*arrays, w_one)


def exclusive_rank(hits):
    rows = hits.shape[1]
    earlier = (jnp.arange(rows)[:, None] < jnp.arange(rows)[None, :]).astype(BF16)
    return jnp.dot(hits.astype(BF16), earlier, preferred_element_type=F32)


def dispatch_gather(tokens, out_grad, routes, probs, w_one, cap):
    tok_rows, width = tokens.shape
    top = routes.shape[1]
    me = lax.axis_index("expert").astype(F32)
    table = jnp.concatenate([routes.T.astype(BF16), probs.T], axis=0)
    table = jnp.pad(table, ((0, -2 * top % 16), (0, 0)))
    table, rows_x, rows_dy, proj = gather_all(
        lax.axis_size("expert"), cap, top, w_one, table, tokens, out_grad
    )
    table = table.astype(F32)
    mine = table[:, :top] == me
    hits = jnp.any(mine, axis=1)
    prob = jnp.sum(jnp.where(mine, table[:, top : 2 * top], 0.0), axis=1)
    rank = exclusive_rank(hits)
    place = (rank[:, None, :] == jnp.arange(cap, dtype=F32)[None, :, None]) & hits[:, None, :]
    rows_p = jnp.sum(jnp.where(place, prob[:, None, :], 0.0), axis=2).reshape(-1)
    return rows_x, rows_dy, rows_p, proj


def dispatch_exchange(tokens, out_grad, probs, slot, experts, cap):
    tok_rows, width = tokens.shape
    top = slot.shape[1]
    flat = slot.reshape(-1)
    slot_hit = flat[:, None] == jnp.arange(experts * cap, dtype=jnp.int32)[None, :]
    filled = jnp.any(slot_hit, axis=0)
    owner = jnp.sum(jnp.where(slot_hit, jnp.arange(flat.shape[0], dtype=jnp.int32)[:, None], 0), axis=0)
    source = owner // top
    zero = jnp.zeros((), BF16)

    def move(rows):
        return lax.all_to_all(rows, "expert", split_axis=0, concat_axis=0, tiled=True)

    send_x = jnp.where(filled[:, None], tokens[source], zero).reshape(experts, cap, width)
    send_dy = jnp.where(filled[:, None], out_grad[source], zero).reshape(experts, cap, width)
    send_p = jnp.where(filled, probs.reshape(-1)[owner], zero).reshape(experts, cap)
    return (
        move(send_x).reshape(-1, width),
        move(send_dy).reshape(-1, width),
        move(send_p).reshape(-1).astype(F32),
    )


def swap(value, flip):
    return lax.ppermute(value, "dp", [(i, i ^ flip) for i in range(4)])


def square_first(piece):
    got = []
    for rest in (True, False):
        for half, side in ((0, 1), (1, 2)):
            flip = 3 if rest else side
            got.append(swap(piece(flip, half).astype(BF16), side))
    return got


def square_second(piece, got):
    sent = []
    for half, side in ((0, 2), (1, 1)):
        total = (piece(side, half) + got[half].astype(F32)).astype(BF16)
        sent.append(swap(total, side))
    return [
        (piece(0, half) + got[2 + half].astype(F32) + sent[half].astype(F32)).astype(BF16)
        for half in range(2)
    ]


def shards(tokens, out_grad, routes, probs, w_in, w_out):
    tok_rows, width = tokens.shape
    top = routes.shape[1]
    n_groups = lax.axis_size("expert")
    experts = n_groups * w_in.shape[0]
    hidden = w_out.shape[1]
    cap = 4 * tok_rows * top // (3 * experts)
    w_one, w_two = w_in[0], w_out[0]

    names = jnp.arange(experts, dtype=jnp.int32)
    named = routes[:, :, None] == names[None, None, :]
    hits = jnp.any(named, axis=1)
    later = (jnp.arange(tok_rows)[:, None] > jnp.arange(tok_rows)[None, :]).astype(BF16)
    rank = jnp.dot(later, hits.astype(BF16), preferred_element_type=F32)
    own_rank = jnp.sum(jnp.where(named, rank[:, None, :], 0.0), axis=2).astype(jnp.int32)
    slot = routes * cap + own_rank

    if experts <= 16:
        rows_x, rows_dy, rows_p, proj = dispatch_gather(tokens, out_grad, routes, probs, w_one, cap)
    else:
        rows_x, rows_dy, rows_p = dispatch_exchange(tokens, out_grad, probs, slot, experts, cap)
        proj = jnp.dot(rows_x, w_one, preferred_element_type=F32)
    rows_p = rows_p[:, None]
    gate, upper = proj[:, :hidden], proj[:, hidden:]
    sig = jax.nn.sigmoid(gate)
    act = gate * sig
    hid = (act * upper).astype(BF16)
    scaled = (rows_p * hid.astype(F32)).astype(BF16)
    replicas = lax.axis_size("dp")
    part = width // replicas
    at = lax.axis_index("dp")
    contract = (((0,), (0,)), ((), ()))

    def piece_two(flip, half):
        cut = lax.dynamic_slice_in_dim(rows_dy, (at ^ flip) * part, part, axis=1)
        units = scaled[:, half * (hidden // 2) : (half + 1) * (hidden // 2)]
        return lax.dot_general(units, cut, contract, preferred_element_type=F32)

    if replicas == 4:
        first_two = square_first(piece_two)
    else:
        grad_two = lax.dot_general(scaled, rows_dy, contract, preferred_element_type=F32).astype(BF16)
        share_two = lax.psum_scatter(grad_two, "dp", scatter_dimension=1, tiled=True)

    back = lax.dot_general(rows_dy, w_two, (((1,), (1,)), ((), ())), preferred_element_type=F32)
    dprob = jnp.sum(back * hid.astype(F32), axis=1).astype(BF16)
    hid_grad = rows_p * back
    proj_grad = jnp.concatenate(
        [hid_grad * upper * (sig * (1.0 + gate * (1.0 - sig))), hid_grad * act], axis=1
    ).astype(BF16)

    def piece_one(flip, half):
        cut = lax.dynamic_slice_in_dim(rows_x, (at ^ flip) * part, part, axis=1)
        units = proj_grad[:, half * hidden : (half + 1) * hidden]
        return lax.dot_general(cut, units, contract, preferred_element_type=F32)

    if replicas == 4:
        first_one = square_first(piece_one)
        second_two = square_second(piece_two, first_two)
        second_one = square_second(piece_one, first_one)
        share_two = jnp.concatenate(second_two, axis=0)
        share_one = jnp.concatenate(second_one, axis=1)
    else:
        grad_one = lax.dot_general(rows_x, proj_grad, contract, preferred_element_type=F32).astype(BF16)
        share_one = lax.psum_scatter(grad_one, "dp", scatter_dimension=0, tiled=True)

    row_grad = lax.dot_general(
        proj_grad, w_one, (((1,), (1,)), ((), ())), preferred_element_type=F32
    ).astype(BF16)
    back_x = lax.all_to_all(
        row_grad.reshape(n_groups, cap, width), "expert", split_axis=0, concat_axis=0, tiled=True
    ).reshape(experts * cap, width)
    back_p = lax.all_to_all(
        dprob.reshape(n_groups, cap), "expert", split_axis=0, concat_axis=0, tiled=True
    ).reshape(-1)
    slots = jnp.arange(experts * cap, dtype=jnp.int32)
    held = slot[:, :, None] == slots[None, None, :]
    prob_grad = jnp.sum(jnp.where(held, back_p.astype(F32), 0.0), axis=2).astype(BF16)
    token_grad = jnp.dot(
        jnp.any(held, axis=1).astype(BF16), back_x, preferred_element_type=F32
    ).astype(BF16)
    return token_grad, prob_grad, share_one[None], share_two[None]


def solution(mesh):
    return jax.shard_map(
        shards,
        mesh=mesh,
        in_specs=(
            P(("dp", "expert"), None),
            P(("dp", "expert"), None),
            P(("dp", "expert"), None),
            P(("dp", "expert"), None),
            P("expert", None, None),
            P("expert", None, None),
        ),
        out_specs=(
            P(("dp", "expert"), None),
            P(("dp", "expert"), None),
            P("expert", "dp", None),
            P("expert", None, "dp"),
        ),
        check_vma=False,
    )
```

```python
import jax
import jax.numpy as jnp
from jax import lax
from jax.experimental import pallas as pl
from jax.experimental.pallas import tpu as pltpu
from jax.sharding import PartitionSpec as P

F32 = jnp.float32
BF16 = jnp.bfloat16


def gather_kernel(n, cap, top, *refs):
    count = 3
    ins, w_hbm = refs[:count], refs[count]
    table_out, rows_x, rows_dy, proj = refs[count + 1 : count + 5]
    all_x, all_dy, w_vmem, w_sem, own_sem, send_sem, recv_sem = refs[count + 5 :]
    outs = (table_out, all_x, all_dy)
    load_w = pltpu.make_async_copy(w_hbm, w_vmem, w_sem)
    load_w.start()
    chips = n // 2
    me = lax.axis_index("expert")
    z, core = me // 2, me % 2
    ways = (
        (me - core + 1 - core, None),
        (me + 2, z < chips - 1),
        (me - 2, z > 0),
    )

    def guarded(ok, body):
        if ok is None:
            body()
        else:
            pl.when(ok)(body)

    barrier = pltpu.get_barrier_semaphore()
    for target, ok in ways:
        guarded(ok, lambda target=target: pl.semaphore_signal(
            barrier, inc=1, device_id={"expert": target}, device_id_type=pl.DeviceIdType.MESH
        ))
    peers = 1 + (z < chips - 1).astype(jnp.int32) + (z > 0).astype(jnp.int32)
    pl.semaphore_wait(barrier, peers)

    def copy(a, slot, hop, way):
        source = ins[a] if hop is None else outs[a].at[slot]
        return pltpu.make_async_remote_copy(
            src_ref=source,
            dst_ref=outs[a].at[slot],
            send_sem=send_sem.at[a, 0 if hop is None else hop, way],
            recv_sem=recv_sem.at[a, slot],
            device_id={"expert": ways[way][0]},
            device_id_type=pl.DeviceIdType.MESH,
        )

    def locals_():
        return [pltpu.make_async_copy(ins[a], outs[a].at[me], own_sem.at[a]) for a in range(count)]

    for c in locals_():
        c.start()
    hops = []
    for step in range(1, chips):
        hops.append((2 * step - 1, me - 2 * step, z - step >= 0, 1))
        hops.append((2 * step, me + 2 * step, z + step < chips, 2))
    def pick(rows_in, rows_out):
        tok = rows_in.shape[1]
        earlier = (
            lax.broadcasted_iota(jnp.int32, (tok, tok), 0) < lax.broadcasted_iota(jnp.int32, (tok, tok), 1)
        )
        earlier = jnp.where(earlier, 1.0, 0.0).astype(BF16)
        order = lax.broadcasted_iota(jnp.int32, (cap, tok), 0).astype(F32)

        def one(b, carry):
            named = table_out[b].astype(F32)
            hit = jnp.zeros((1, tok), F32)
            for k in range(top):
                hit = hit + jnp.where(named[k : k + 1] == me.astype(F32), 1.0, 0.0)
            rank = jnp.dot(
                jnp.broadcast_to(hit, (16, tok)).astype(BF16), earlier, preferred_element_type=F32
            )[0:1]
            place = jnp.where(order == rank, 1.0, 0.0) * hit
            rows_out[pl.ds(pl.multiple_of(b * cap, cap), cap), :] = jnp.dot(
                place.astype(BF16), rows_in[b], preferred_element_type=F32
            ).astype(BF16)
            return carry

        lax.fori_loop(0, n, one, 0)

    def send_own(a):
        for way in (1, 2, 0):
            guarded(ways[way][1], lambda a=a, way=way: copy(a, me, None, way).start())

    def pass_on(a, first, last):
        for hop, slot, here, way in hops[first:last]:

            def relay(a=a, hop=hop, slot=slot, way=way):
                copy(a, slot, hop, way).wait_recv()
                pl.when(ways[way][1])(lambda: copy(a, slot, hop, way).start())
                copy(a, slot, hop, 0).start()

            pl.when(here)(relay)

    def finish(a):
        for chip in range(chips):
            copy(a, 2 * chip + 1 - core, 0, 0).wait_recv()

    send_own(0)
    send_own(1)
    pass_on(0, 0, None)
    pass_on(1, 0, -2)
    send_own(2)
    pass_on(1, -2, None)
    for c in locals_():
        c.wait()
    finish(0)
    finish(1)
    load_w.wait()
    tile = 256
    steps = proj.shape[1] // tile
    width = steps // len(hops) if steps >= len(hops) else 0

    def columns(first, last):
        def one(i, carry):
            at = pl.ds(pl.multiple_of(i * tile, tile), tile)
            proj[:, at] = jnp.dot(rows_x[...], w_vmem[:, at], preferred_element_type=F32)
            return carry

        lax.fori_loop(first, last, one, 0)

    pick(all_x, rows_x)
    for i, (hop, slot, here, way) in enumerate(hops):

        def relay(hop=hop, slot=slot, way=way):
            copy(2, slot, hop, way).wait_recv()
            pl.when(ways[way][1])(lambda: copy(2, slot, hop, way).start())
            copy(2, slot, hop, 0).start()

        pl.when(here)(relay)
        columns(i * width, (i + 1) * width if i < len(hops) - 1 else steps)
    finish(2)
    pick(all_dy, rows_dy)
    for a in range(count):
        for way in range(3):
            guarded(ways[way][1], lambda a=a, way=way: copy(a, me, None, way).wait_send())
        for hop, slot, here, way in hops:

            def drain(a=a, hop=hop, slot=slot, way=way):
                pl.when(ways[way][1])(lambda: copy(a, slot, hop, way).wait_send())
                copy(a, slot, hop, 0).wait_send()

            pl.when(here)(drain)


def gather_all(n, cap, top, w_one, *arrays):
    table, rows = arrays[:2]
    vmem, width = pl.BlockSpec(memory_space=pltpu.VMEM), rows.shape[1]
    return pl.pallas_call(
        lambda *refs: gather_kernel(n, cap, top, *refs),
        out_shape=[
            jax.ShapeDtypeStruct((n,) + table.shape, BF16),
            jax.ShapeDtypeStruct((n * cap, width), BF16),
            jax.ShapeDtypeStruct((n * cap, width), BF16),
            jax.ShapeDtypeStruct((n * cap, w_one.shape[1]), F32),
        ],
        in_specs=[vmem] * 3 + [pl.BlockSpec(memory_space=pl.ANY)],
        out_specs=[vmem] * 4,
        scratch_shapes=[
            pltpu.VMEM((n,) + rows.shape, BF16),
            pltpu.VMEM((n,) + rows.shape, BF16),
            pltpu.VMEM(w_one.shape, BF16),
            pltpu.SemaphoreType.DMA,
            pltpu.SemaphoreType.DMA((3,)),
            pltpu.SemaphoreType.DMA((3, n - 1, 3)),
            pltpu.SemaphoreType.DMA((3, n)),
        ],
        compiler_params=pltpu.CompilerParams(
            collective_id=0, has_side_effects=True, vmem_limit_bytes=48 * 1024 * 1024
        ),
    )(*arrays, w_one)


def exclusive_rank(hits):
    rows = hits.shape[1]
    earlier = (jnp.arange(rows)[:, None] < jnp.arange(rows)[None, :]).astype(BF16)
    return jnp.dot(hits.astype(BF16), earlier, preferred_element_type=F32)


def dispatch_gather(tokens, out_grad, routes, probs, w_one, cap):
    tok_rows, width = tokens.shape
    top = routes.shape[1]
    me = lax.axis_index("expert").astype(F32)
    table = jnp.concatenate([routes.T.astype(BF16), probs.T], axis=0)
    table = jnp.pad(table, ((0, -2 * top % 16), (0, 0)))
    table, rows_x, rows_dy, proj = gather_all(
        lax.axis_size("expert"), cap, top, w_one, table, tokens, out_grad
    )
    table = table.astype(F32)
    mine = table[:, :top] == me
    hits = jnp.any(mine, axis=1)
    prob = jnp.sum(jnp.where(mine, table[:, top : 2 * top], 0.0), axis=1)
    rank = exclusive_rank(hits)
    place = (rank[:, None, :] == jnp.arange(cap, dtype=F32)[None, :, None]) & hits[:, None, :]
    rows_p = jnp.sum(jnp.where(place, prob[:, None, :], 0.0), axis=2).reshape(-1)
    return rows_x, rows_dy, rows_p, proj


def dispatch_exchange(tokens, out_grad, probs, slot, experts, cap):
    tok_rows, width = tokens.shape
    top = slot.shape[1]
    flat = slot.reshape(-1)
    slot_hit = flat[:, None] == jnp.arange(experts * cap, dtype=jnp.int32)[None, :]
    filled = jnp.any(slot_hit, axis=0)
    owner = jnp.sum(jnp.where(slot_hit, jnp.arange(flat.shape[0], dtype=jnp.int32)[:, None], 0), axis=0)
    source = owner // top
    zero = jnp.zeros((), BF16)

    def move(rows):
        return lax.all_to_all(rows, "expert", split_axis=0, concat_axis=0, tiled=True)

    send_x = jnp.where(filled[:, None], tokens[source], zero).reshape(experts, cap, width)
    send_dy = jnp.where(filled[:, None], out_grad[source], zero).reshape(experts, cap, width)
    send_p = jnp.where(filled, probs.reshape(-1)[owner], zero).reshape(experts, cap)
    return (
        move(send_x).reshape(-1, width),
        move(send_dy).reshape(-1, width),
        move(send_p).reshape(-1).astype(F32),
    )


def swap(value, flip):
    return lax.ppermute(value, "dp", [(i, i ^ flip) for i in range(4)])


def square_first(piece):
    got = []
    for rest in (True, False):
        for half, side in ((0, 1), (1, 2)):
            flip = 3 if rest else side
            got.append(swap(piece(flip, half).astype(BF16), side))
    return got


def square_second(piece, got):
    sent = []
    for half, side in ((0, 2), (1, 1)):
        total = (piece(side, half) + got[half].astype(F32)).astype(BF16)
        sent.append(swap(total, side))
    return [
        (piece(0, half) + got[2 + half].astype(F32) + sent[half].astype(F32)).astype(BF16)
        for half in range(2)
    ]


def shards(tokens, out_grad, routes, probs, w_in, w_out):
    tok_rows, width = tokens.shape
    top = routes.shape[1]
    n_groups = lax.axis_size("expert")
    experts = n_groups * w_in.shape[0]
    hidden = w_out.shape[1]
    cap = 4 * tok_rows * top // (3 * experts)
    w_one, w_two = w_in[0], w_out[0]

    names = jnp.arange(experts, dtype=jnp.int32)
    named = routes[:, :, None] == names[None, None, :]
    hits = jnp.any(named, axis=1)
    later = (jnp.arange(tok_rows)[:, None] > jnp.arange(tok_rows)[None, :]).astype(BF16)
    rank = jnp.dot(later, hits.astype(BF16), preferred_element_type=F32)
    own_rank = jnp.sum(jnp.where(named, rank[:, None, :], 0.0), axis=2).astype(jnp.int32)
    slot = routes * cap + own_rank

    if experts <= 16:
        rows_x, rows_dy, rows_p, proj = dispatch_gather(tokens, out_grad, routes, probs, w_one, cap)
    else:
        rows_x, rows_dy, rows_p = dispatch_exchange(tokens, out_grad, probs, slot, experts, cap)
        proj = jnp.dot(rows_x, w_one, preferred_element_type=F32)
    rows_p = rows_p[:, None]
    gate, upper = proj[:, :hidden], proj[:, hidden:]
    sig = jax.nn.sigmoid(gate)
    act = gate * sig
    hid = (act * upper).astype(BF16)
    scaled = (rows_p * hid.astype(F32)).astype(BF16)
    replicas = lax.axis_size("dp")
    part = width // replicas
    at = lax.axis_index("dp")
    contract = (((0,), (0,)), ((), ()))

    def piece_two(flip, half):
        cut = lax.dynamic_slice_in_dim(rows_dy, (at ^ flip) * part, part, axis=1)
        units = scaled[:, half * (hidden // 2) : (half + 1) * (hidden // 2)]
        return lax.dot_general(units, cut, contract, preferred_element_type=F32)

    if replicas == 4:
        first_two = square_first(piece_two)
    else:
        grad_two = lax.dot_general(scaled, rows_dy, contract, preferred_element_type=F32).astype(BF16)
        share_two = lax.psum_scatter(grad_two, "dp", scatter_dimension=1, tiled=True)

    back = lax.dot_general(rows_dy, w_two, (((1,), (1,)), ((), ())), preferred_element_type=F32)
    dprob = jnp.sum(back * hid.astype(F32), axis=1).astype(BF16)
    hid_grad = rows_p * back
    proj_grad = jnp.concatenate(
        [hid_grad * upper * (sig * (1.0 + gate * (1.0 - sig))), hid_grad * act], axis=1
    ).astype(BF16)

    def piece_one(flip, half):
        cut = lax.dynamic_slice_in_dim(rows_x, (at ^ flip) * part, part, axis=1)
        units = proj_grad[:, half * hidden : (half + 1) * hidden]
        return lax.dot_general(cut, units, contract, preferred_element_type=F32)

    if replicas == 4:
        first_one = square_first(piece_one)
        second_two = square_second(piece_two, first_two)
        second_one = square_second(piece_one, first_one)
        share_two = jnp.concatenate(second_two, axis=0)
        share_one = jnp.concatenate(second_one, axis=1)
    else:
        grad_one = lax.dot_general(rows_x, proj_grad, contract, preferred_element_type=F32).astype(BF16)
        share_one = lax.psum_scatter(grad_one, "dp", scatter_dimension=0, tiled=True)

    row_grad = lax.dot_general(
        proj_grad, w_one, (((1,), (1,)), ((), ())), preferred_element_type=F32
    ).astype(BF16)
    back_x = lax.all_to_all(
        row_grad.reshape(n_groups, cap, width), "expert", split_axis=0, concat_axis=0, tiled=True
    ).reshape(experts * cap, width)
    back_p = lax.all_to_all(
        dprob.reshape(n_groups, cap), "expert", split_axis=0, concat_axis=0, tiled=True
    ).reshape(-1)
    slots = jnp.arange(experts * cap, dtype=jnp.int32)
    held = slot[:, :, None] == slots[None, None, :]
    prob_grad = jnp.sum(jnp.where(held, back_p.astype(F32), 0.0), axis=2).astype(BF16)
    token_grad = jnp.dot(
        jnp.any(held, axis=1).astype(BF16), back_x, preferred_element_type=F32
    ).astype(BF16)
    return token_grad, prob_grad, share_one[None], share_two[None]


def solution(mesh):
    return jax.shard_map(
        shards,
        mesh=mesh,
        in_specs=(
            P(("dp", "expert"), None),
            P(("dp", "expert"), None),
            P(("dp", "expert"), None),
            P(("dp", "expert"), None),
            P("expert", None, None),
            P("expert", None, None),
        ),
        out_specs=(
            P(("dp", "expert"), None),
            P(("dp", "expert"), None),
            P("expert", "dp", None),
            P("expert", None, "dp"),
        ),
        check_vma=False,
    )
```
